32 devices in a mesh: dp: 2 (over y), expert: 4 (over x, core), tensor: 4 (over z).
Axes of the slice: x: 2, y: 2, z: 4, core: 2. Of those that a mesh axis runs over, the one named last changes fastest.
Arguments:
- ssm_in: bfloat16 [1024, 4096], P('dp', 'tensor'), may hold values from -6 to 6
- gate_z: bfloat16 [1024, 4096], P('dp', 'tensor'), may hold values from -6 to 6
- b_proj: bfloat16 [1024, 128], P('dp'), may hold values from -6 to 6
- c_proj: bfloat16 [1024, 128], P('dp'), may hold values from -6 to 6
- step_size: float32 [1024, 64], P('dp', 'tensor'), may hold values from 0.25 to 2
- decay_rate: float32 [64], P('tensor'), may hold values from 0.00024414062 to 0.0333333333
- norm_gain: float32 [4096], P('tensor'), may hold values from 0.5 to 1.5
- w_out: bfloat16 [4096, 4096], P('tensor', 'expert'), may hold values from -0.09375 to 0.09375
- residual: bfloat16 [1024, 4096], P(('dp', 'tensor'), 'expert'), may hold values from -6 to 6
- moe_gain: float32 [4096], P('expert'), may hold values from 0.5 to 1.5
- expert_ids: int32 [1024, 10], P(('dp', 'tensor')), may hold values from 0 to 63, all different within a row; in each aligned block of 128 rows (0 to 127, 128 to 255, ...) at most 28 rows name the same one
- route_weight: bfloat16 [1024, 10], P(('dp', 'tensor')), may hold values from 0.099609375 to 0.5
- w_gate: bfloat16 [64, 4096, 896], P(('dp', 'tensor'), 'expert'), may hold values from -0.09375 to 0.09375
- w_up: bfloat16 [64, 4096, 896], P(('dp', 'tensor'), 'expert'), may hold values from -0.09375 to 0.09375
- w_down: bfloat16 [64, 896, 4096], P(('dp', 'tensor'), None, 'expert'), may hold values from -0.1875 to 0.1875
Outputs:
- layer_out: bfloat16 [1024, 4096], P(('dp', 'tensor'), 'expert')
The draws below stay inside these ranges and needn't reach their ends.
Inputs may be any that keep to these rules, and one draw needn't show every extreme that they name: `expert_ids`: each row names 10 different experts. In each aligned block of 128 rows no expert is named by more than 28 rows, a bound that some block reaches.
All inputs are finite; a program needn't handle non-finite values.
Results may differ from the reference program's by a relative error of at most 0.019.
Values may be sent and summed in bfloat16 or wider, within the bound.
No kernel may reach another device: no remote copies, remote signals or barrier semaphores. Data moves between devices by JAX's collectives and lax.ppermute only.
A program may use at most 128 MiB of HBM per device.

```python
import math
import jax
import jax.numpy as jnp
import numpy as np
from jax import lax

D = 4096
F = 896
HEADS = 64
HEAD_DIM = 64
STATE = 128
EXPERTS = 64
TOPK = 10
TOK_DP = 512
TOKENS = 1024
TOK_SRC = 128
SLOT = 28


def draw_decay_rate(key, part):
    pick = jax.random.uniform(jax.random.fold_in(key, 11), (HEADS,))
    fast = pick < 0.5
    quick = jax.random.uniform(jax.random.fold_in(key, 12), (HEADS,), minval=1.0 / 50.0, maxval=1.0 / 30.0)
    slow = jnp.exp(jax.random.uniform(jax.random.fold_in(key, 13), (HEADS,), minval=math.log(0.25), maxval=math.log(0.5))) / TOKENS
    return jnp.where(fast, quick, slow).astype(jnp.float32)


def draw_step_size(key, part):
    blocks = TOKENS // TOK_DP
    base = jax.random.uniform(jax.random.fold_in(key, 21), (blocks, TOK_DP, HEADS), minval=0.5, maxval=1.0)
    factor = jnp.exp(jax.random.uniform(jax.random.fold_in(key, 22), (blocks, 1, HEADS), minval=math.log(0.5), maxval=math.log(2.0)))
    return (base * factor).reshape(TOKENS, HEADS).astype(jnp.float32)


def shard_levels(own_key, dims, split, smallest, top_value):
    level = 1.0
    for dim, shards_of in split:
        draws = jax.random.uniform(jax.random.fold_in(jax.random.fold_in(own_key, 6), dim), (shards_of,), jnp.float32, smallest / len(split), top_value / len(split))
        level = level * jnp.repeat(jnp.exp(draws), dims[dim] // shards_of).reshape((-1,) + (1,) * (len(dims) - 1 - dim))
    return level


def routed_block(own_key, own, number, rows, count, top, most, skew):
    sequence = jax.random.permutation(own_key, count)
    crowded, ordinary = shares(count, rows * top, most, skew, True), shares(count, rows * top, most, skew, False)
    places = jnp.arange(count)

    def named(sizes, offset_by):
        used = int((sizes > 0).sum())
        fixed = max(1, used // 4)
        passed = fixed + (places - fixed + offset_by * (used - fixed)) % max(1, count - fixed)
        return jnp.zeros((count,), jnp.int32).at[sequence[jnp.where(places < fixed, places, passed)]].set(jnp.asarray(sizes, jnp.int32))

    sizes = jnp.where(number % 4 == 0, named(crowded, number // 4), named(ordinary, number - number // 4 - 1))
    mixed = jax.random.permutation(jax.random.fold_in(own, 3), count)
    donor, taker = mixed[0:count // 2 * 2:2], mixed[1:count // 2 * 2:2]
    room = jnp.minimum(sizes[donor] - 1, most - sizes[taker]) // 2
    room = jnp.where((donor == sequence[0]) | (taker == sequence[0]) | (sizes[taker] == 0), 0, jnp.maximum(room, 0))
    passed = jax.random.randint(jax.random.fold_in(own, 4), (count // 2,), 0, 1 << 20) % (room + 1)
    sizes = sizes.at[donor].add(-passed).at[taker].add(passed)
    members = jnp.searchsorted(jnp.cumsum(sizes), jnp.arange(rows * top), side="right").astype(jnp.int32)
    table = members.reshape(top, rows).T
    table = table[jax.random.permutation(jax.random.fold_in(own, 1), rows)]
    offset_by = jax.random.randint(jax.random.fold_in(own, 2), (rows, 1), 0, top)
    return jnp.take_along_axis(table, (jnp.arange(top)[None, :] + offset_by) % top, axis=1)


def shares(count, total, reach, slope, full):
    portions = [(1 << 20) // math.isqrt(standing ** slope) + 1 for standing in range(1, count + 1)]
    largest = reach if full else min(reach, max(-(-total // count), total * portions[0] // sum(portions)))
    least = 1 if total - largest >= count - 1 else 0
    counts, spare = [largest] + [least] * (count - 1), total - largest - least * (count - 1)
    while spare > 0:
        candidates = [i for i in range(1, count) if counts[i] < largest] or [i for i in range(1, count) if counts[i] < reach]
        pool, left = sum([portions[i] for i in candidates]), spare
        for i in candidates:
            addition = min(reach - counts[i], max(1, left * portions[i] // pool), spare)
            counts[i] = counts[i] + addition
            spare = spare - addition
    return np.array(counts)


def centred(key, extent, deviation, bound, shards=(), kind=jnp.bfloat16):
    gain = shard_levels(key, extent, shards, -0.22, 0.18) if shards else 1.0
    entries = jax.random.normal(key, extent, jnp.float32) * deviation * gain
    return jnp.minimum(jnp.maximum(entries, -bound), bound).astype(kind)


def setup_inputs(seed: int = 0) -> dict:
    seeds = jax.random.split(jax.random.key(seed), 16)
    ssm_in = centred(seeds[0], (TOKENS, HEADS * HEAD_DIM), 1.0, 6.0, ((0, 2), (1, 4)))
    gate_z = centred(seeds[1], (TOKENS, HEADS * HEAD_DIM), 1.0, 6.0, ((0, 2), (1, 4)))
    b_proj = centred(seeds[2], (TOKENS, STATE), 1.0, 6.0, ((0, 2),))
    c_proj = centred(seeds[3], (TOKENS, STATE), 1.0, 6.0, ((0, 2),))
    step_size = draw_step_size(jax.random.fold_in(seeds[15], 71), 0)
    decay_rate = draw_decay_rate(jax.random.fold_in(seeds[15], 71), 0)
    norm_gain = jnp.clip(1.0 + 0.1 * jax.random.normal(seeds[6], (HEADS * HEAD_DIM,), jnp.float32), 0.5, 1.5)
    w_out = centred(seeds[7], (HEADS * HEAD_DIM, D), (HEADS * HEAD_DIM) ** -0.5, 0.09375, ((0, 4), (1, 4)))
    residual = centred(seeds[8], (TOKENS, D), 1.0, 6.0, ((0, 8), (1, 4)))
    moe_gain = jnp.clip(1.0 + 0.1 * jax.random.normal(seeds[9], (D,), jnp.float32), 0.5, 1.5)
    expert_ids_keys = jax.random.split(jax.random.fold_in(seeds[10], 1), TOKENS // TOK_SRC)
    expert_ids_turns = jax.random.permutation(jax.random.fold_in(seeds[10], 3), TOKENS // TOK_SRC)
    expert_ids = jax.vmap(lambda own, number: routed_block(jax.random.fold_in(seeds[10], 2), own, number, TOK_SRC, EXPERTS, TOPK, SLOT, 2))(expert_ids_keys, expert_ids_turns).reshape((TOKENS, TOPK))
    route_weight = jnp.clip(0.099609375 + 0.40039062 * jax.random.uniform(seeds[11], (TOKENS, TOPK), jnp.float32) ** shard_levels(seeds[11], (TOKENS, TOPK), ((0, 8),), -0.2, 0.2), 0.099609375, 0.5).astype(jnp.bfloat16)
    w_gate = centred(seeds[12], (EXPERTS, D, F), D ** -0.5, 0.09375, ((0, 8), (1, 4)))
    w_up = centred(seeds[13], (EXPERTS, D, F), D ** -0.5, 0.09375, ((0, 8), (1, 4)))
    w_down = centred(seeds[14], (EXPERTS, F, D), F ** -0.5, 0.1875, ((0, 8), (2, 4)))
    return dict(ssm_in=ssm_in, gate_z=gate_z, b_proj=b_proj, c_proj=c_proj, step_size=step_size, decay_rate=decay_rate, norm_gain=norm_gain, w_out=w_out, residual=residual, moe_gain=moe_gain, expert_ids=expert_ids, route_weight=route_weight, w_gate=w_gate, w_up=w_up, w_down=w_down)


EPSILON = 1e-05

def silu_of(value):
    return value / (1.0 + jnp.exp(-value))

def reference(ssm_in, gate_z, b_proj, c_proj, step_size, decay_rate, norm_gain, w_out, residual, moe_gain, expert_ids, route_weight, w_gate, w_up, w_down):
    seq_len = ssm_in.shape[0]
    heads_in = ssm_in.astype(jnp.float32).reshape(seq_len, HEADS, HEAD_DIM)
    b_float = b_proj.astype(jnp.float32)
    c_float = c_proj.astype(jnp.float32)
    log_decay = -step_size * decay_rate[None, :]

    def advance(state, inputs):
        x_now, b_now, c_now, step_now, decay_now = inputs
        update = (step_now[:, None] * x_now)[:, :, None] * b_now[None, None, :]
        state = jnp.exp(decay_now)[:, None, None] * state + update
        output = jnp.einsum('hpn,n->hp', state, c_now, precision=lax.Precision.HIGHEST)
        return (state, output)
    start_state = jnp.zeros((HEADS, HEAD_DIM, STATE), jnp.float32)
    _, scan_out = lax.scan(advance, start_state, (heads_in, b_float, c_float, step_size, log_decay))
    scan_out = scan_out.reshape(seq_len, HEADS * HEAD_DIM)
    gated_out = scan_out * silu_of(gate_z.astype(jnp.float32))
    head_scale = lax.rsqrt(lax.optimization_barrier(jnp.mean(gated_out * gated_out, axis=1)) + EPSILON)
    scaled = (gated_out * norm_gain[None, :]).astype(jnp.bfloat16)
    mamba_out = jnp.dot(scaled, w_out, preferred_element_type=jnp.float32) * head_scale[:, None]
    stream = (residual.astype(jnp.float32) + mamba_out).astype(jnp.bfloat16)
    stream_f = stream.astype(jnp.float32)
    model_scale = lax.rsqrt(lax.optimization_barrier(jnp.mean(stream_f * stream_f, axis=1)) + EPSILON)
    normed = (stream_f * model_scale[:, None] * moe_gain[None, :]).astype(jnp.bfloat16)
    sources = seq_len // TOK_SRC
    expert_grid = jnp.arange(EXPERTS, dtype=jnp.int32)
    per_token = lax.optimization_barrier(jnp.sum((expert_ids[:, :, None] == expert_grid[None, None, :]).astype(jnp.int32), axis=1))
    blocked = per_token.reshape(sources, TOK_SRC, EXPERTS)
    earlier = (jnp.cumsum(blocked, axis=1) - blocked).reshape(seq_len, EXPERTS)
    slot_index = jnp.take_along_axis(earlier, expert_ids, axis=1)
    token_grid = jnp.arange(seq_len, dtype=jnp.int32)
    column = ((token_grid // TOK_SRC)[:, None] * SLOT + slot_index).astype(jnp.int32)
    capacity = sources * SLOT
    token_table = jnp.zeros((EXPERTS, capacity), jnp.int32).at[expert_ids, column].set(jnp.broadcast_to(token_grid[:, None], expert_ids.shape))
    filled = jnp.zeros((EXPERTS, capacity), jnp.bfloat16).at[expert_ids, column].set(jnp.ones(expert_ids.shape, jnp.bfloat16))

    def run_expert(packed):
        index_row, filled_row, gate_w, up_w, down_w = packed
        grouped = normed[index_row] * filled_row[:, None]
        gate = jnp.dot(grouped, gate_w, preferred_element_type=jnp.float32)
        up_val = jnp.dot(grouped, up_w, preferred_element_type=jnp.float32)
        activated = (silu_of(gate) * up_val).astype(jnp.bfloat16)
        return jnp.dot(activated, down_w, preferred_element_type=jnp.float32).astype(jnp.bfloat16)
    expert_out = lax.map(run_expert, (token_table, filled, w_gate, w_up, w_down))
    picked = expert_out[expert_ids, column]
    blended = jnp.einsum('tk,tkd->td', route_weight.astype(jnp.float32), picked.astype(jnp.float32), precision=lax.Precision.HIGHEST)
    return (stream_f + blended).astype(jnp.bfloat16)
```

```python
import functools

import jax
import jax.numpy as jnp
from jax import lax
from jax.experimental import pallas as pl
from jax.experimental.pallas import tpu as pltpu
from jax.sharding import PartitionSpec as P

EPSILON = 1e-05
F32, BF16 = jnp.float32, jnp.bfloat16


def dot(a, b, dims=((1,), (0,))):
    return lax.dot_general(a, b, (dims, ((), ())), preferred_element_type=F32)


def iota(shape, dim, dtype=jnp.int32):
    return lax.broadcasted_iota(jnp.int32, shape, dim).astype(dtype)


def silu_of(value):
    return value / (1.0 + jnp.exp(-value))


def split3(value):
    hi = value.astype(BF16)
    rest = value - hi.astype(F32)
    mid = rest.astype(BF16)
    return hi, mid, (rest - mid.astype(F32)).astype(BF16)


def spread(value, head_dim, width, first):
    heads = value.shape[1]
    channel = iota((heads, width), 1) + first
    head = iota((heads, width), 0)
    low = head * head_dim
    member = ((channel >= low) & (channel < low + head_dim)).astype(F32).astype(BF16)
    return sum(dot(part, member) for part in split3(value))


def row_sums(square):
    ones = jnp.ones((8, square.shape[1]), BF16)
    hi = square.astype(BF16)
    lo = (square - hi.astype(F32)).astype(BF16)
    along = ((1,), (1,))
    return dot(ones, hi, along) + dot(ones, lo, along)


def cost(flops, read):
    return pl.CostEstimate(flops=int(flops), bytes_accessed=int(read), transcendentals=0)


def whole(array):
    return pl.BlockSpec(array.shape, lambda *_: (0,) * len(array.shape))


def scan_in_kernel(head_dim, x_ref, step_ref, rate_ref, b_ref, xt_ref, g_ref, s_ref, d_ref, a_ref):
    tile = pl.program_id(0)
    length = step_ref.shape[0]
    width = x_ref.shape[1]

    @pl.when(tile == 0)
    def _():
        step = step_ref[...]
        log_decay = -step * rate_ref[...]
        shape = (length, length)
        lower = (iota(shape, 0) >= iota(shape, 1)).astype(F32).astype(BF16)
        total = sum(dot(lower, part) for part in split3(log_decay))
        a_ref[...] = step * jnp.exp(-total)
        g_ref[...] = jnp.exp(total)

    first = tile * width
    scaled = x_ref[...].astype(F32) * spread(a_ref[...], head_dim, width, first)
    xt = scaled.astype(BF16)
    xt_ref[...] = xt
    ending = spread(g_ref[length - 8 : length, :], head_dim, width, first)[7:8, :]
    d_ref[...] = jnp.broadcast_to(ending, d_ref.shape)
    s_ref[...] = (dot(b_ref[...], xt, ((0,), (0,))) * ending).astype(BF16)


def scan_in(ssm_in, step_size, decay_rate, b_proj, head_dim):
    length, channels = ssm_in.shape
    heads, state = step_size.shape[1], b_proj.shape[1]
    width = min(256, channels)
    rate = decay_rate.reshape(1, heads)
    column = lambda rows: pl.BlockSpec((rows, width), lambda i: (0, i))
    return pl.pallas_call(
        functools.partial(scan_in_kernel, head_dim),
        name="scan_in",
        grid=(channels // width,),
        in_specs=[column(length), whole(step_size), whole(rate), whole(b_proj)],
        out_specs=[column(length), whole(step_size), column(state), column(8)],
        out_shape=[
            jax.ShapeDtypeStruct((length, channels), BF16),
            jax.ShapeDtypeStruct((length, heads), F32),
            jax.ShapeDtypeStruct((state, channels), BF16),
            jax.ShapeDtypeStruct((8, channels), F32),
        ],
        scratch_shapes=[pltpu.VMEM((length, heads), F32)],
        cost_estimate=cost(2 * length * channels * state, 4 * length * channels),
    )(ssm_in, step_size, rate, b_proj)


def scan_local_kernel(head_dim, c_ref, b_ref, xt_ref, z_ref, g_ref, y_ref, gate_ref, score_ref):
    tile = pl.program_id(0)
    length = c_ref.shape[0]
    width = xt_ref.shape[1]

    @pl.when(tile == 0)
    def _():
        score = dot(c_ref[...], b_ref[...], ((1,), (1,)))
        shape = (length, length)
        causal = iota(shape, 0) >= iota(shape, 1)
        score_ref[...] = jnp.where(causal, score, 0.0).astype(BF16)

    gate = spread(g_ref[...], head_dim, width, tile * width) * silu_of(z_ref[...].astype(F32))
    gate_ref[...] = gate
    y_ref[...] = dot(score_ref[...], xt_ref[...]) * gate


def scan_local(c_proj, b_proj, xt, gate_z, growth, head_dim):
    length, channels = xt.shape
    width = min(256, channels)
    column = pl.BlockSpec((length, width), lambda i: (0, i))
    out = jax.ShapeDtypeStruct((length, channels), F32)
    return pl.pallas_call(
        functools.partial(scan_local_kernel, head_dim),
        name="scan_local",
        grid=(channels // width,),
        in_specs=[whole(c_proj), whole(b_proj), column, column, whole(growth)],
        out_specs=[column, column],
        out_shape=[out, out],
        scratch_shapes=[pltpu.VMEM((length, length), BF16)],
        cost_estimate=cost(2 * length * channels * length, 12 * length * channels),
    )(c_proj, b_proj, xt, gate_z, growth)


def project_kernel(count, order_ref, c_ref, y_ref, gate_ref, s_ref, gain_ref, w_ref, *outs):
    del order_ref
    step = pl.program_id(0)
    gated = y_ref[...] + dot(c_ref[...], s_ref[...]) * gate_ref[...]
    squares = row_sums(gated * gated)
    value = dot((gated * gain_ref[...]).astype(BF16), w_ref[...])
    for k in range(count):

        @pl.when(step == k)
        def _(k=k):
            outs[k][...] = value.astype(outs[k].dtype)
            outs[count + k][...] = squares


def project(order, c_proj, y, gate, incoming, gain, w_out):
    count = order.shape[0]
    length, channels = y.shape
    rows, features = length // count, w_out.shape[1]
    block = lambda cols: pl.BlockSpec((rows, cols), lambda i, order: (order[i], 0))
    values = [
        jax.ShapeDtypeStruct((rows, features), BF16 if k else F32) for k in range(count)
    ]
    squares = [jax.ShapeDtypeStruct((8, rows), F32)] * count
    outs = pl.pallas_call(
        functools.partial(project_kernel, count),
        name="project",
        grid_spec=pltpu.PrefetchScalarGridSpec(
            num_scalar_prefetch=1,
            grid=(count,),
            in_specs=[block(c_proj.shape[1]), block(channels), block(channels)]
            + [whole(incoming), whole(gain), whole(w_out)],
            out_specs=[whole(s) for s in values + squares],
        ),
        out_shape=values + squares,
        cost_estimate=cost(2 * length * channels * features, 12 * length * channels),
    )(order, c_proj, y, gate, incoming, gain, w_out)
    return outs[:count], outs[count:]


def home_kernel(count, channels, *refs):
    values, squares = refs[:count], refs[count : 2 * count]
    residual_ref, gain_ref, stream_ref, sent_ref, model_ref = refs[2 * count :]
    total = sum(ref[...].astype(F32) for ref in values)
    square = sum(ref[...] for ref in squares)
    scale = jnp.transpose(lax.rsqrt(square / channels + EPSILON))[:, 0:1]
    stream = (residual_ref[...].astype(F32) + total * scale).astype(BF16)
    stream_ref[...] = stream
    wide = stream.astype(F32)
    sent_ref[...] = (wide * gain_ref[...]).astype(BF16)
    model_ref[...] = row_sums(wide * wide)


def home(values, squares, residual, gain, channels):
    rows, features = residual.shape
    args = (*values, *squares, residual, gain)
    out = jax.ShapeDtypeStruct((rows, features), BF16)
    model = jax.ShapeDtypeStruct((8, rows), F32)
    return pl.pallas_call(
        functools.partial(home_kernel, len(values), channels),
        name="home",
        in_specs=[whole(a) for a in args],
        out_specs=[whole(out), whole(out), whole(model)],
        out_shape=[out, out, model],
        grid=(1,),
        cost_estimate=cost(rows * features * 10, 16 * rows * features),
    )(*args)


def enter_kernel(blocks, expert_ref, rank_ref, *refs):
    del expert_ref
    tokens = refs[:blocks]
    gate_w, up_w, out_ref, token_ref = refs[blocks:]

    @pl.when(pl.program_id(0) == 0)
    def _():
        rows = tokens[0].shape[0]
        for n, ref in enumerate(tokens):
            token_ref[n * rows : (n + 1) * rows, :] = ref[...]

    slots, hidden = out_ref.shape[1], gate_w.shape[2]
    here = rank_ref[0] == iota((slots, token_ref.shape[0]), 0, F32)
    rows_in = dot(here.astype(F32).astype(BF16), token_ref[...]).astype(BF16)
    out_ref[0, :, :hidden] = dot(rows_in, gate_w[0]).astype(BF16)
    out_ref[0, :, hidden:] = dot(rows_in, up_w[0]).astype(BF16)


def enter(experts, rank, tokens, w_gate, w_up, slots):
    units, _, length = rank.shape
    width, hidden = w_gate.shape[1:]
    weight = pl.BlockSpec((1, width, hidden), lambda u, experts: (experts[u], 0, 0))
    return pl.pallas_call(
        functools.partial(enter_kernel, len(tokens)),
        name="enter",
        grid_spec=pltpu.PrefetchScalarGridSpec(
            num_scalar_prefetch=1,
            grid=(units,),
            in_specs=[pl.BlockSpec((1, 1, length), lambda u, _: (u, 0, 0))]
            + [whole(t) for t in tokens]
            + [weight, weight],
            out_specs=pl.BlockSpec((1, slots, 2 * hidden), lambda u, _: (u, 0, 0)),
            scratch_shapes=[pltpu.VMEM((length, width), BF16)],
        ),
        out_shape=jax.ShapeDtypeStruct((units, slots, 2 * hidden), BF16),
        cost_estimate=cost(4 * units * slots * width * hidden, 4 * units * width * hidden),
    )(experts, rank, *tokens, w_gate, w_up)


def activate_kernel(count, rank_ref, scale_ref, *refs):
    parts, out_ref = refs[:count], refs[count]
    slots, hidden = out_ref.shape[1:]
    here = rank_ref[0] == iota((slots, rank_ref.shape[2]), 0, F32)
    scale = jnp.sum(jnp.where(here, scale_ref[...], 0.0), axis=1, keepdims=True)
    total = sum(ref[0].astype(F32) for ref in parts) * scale
    out_ref[0] = (silu_of(total[:, :hidden]) * total[:, hidden:]).astype(BF16)


def activate(rank, scale, parts):
    units = parts[-1].shape[0]
    slots, double = parts[-1].shape[1:]
    unit = lambda *shape: pl.BlockSpec((1, *shape), lambda u: (u, 0, 0))
    return pl.pallas_call(
        functools.partial(activate_kernel, len(parts)),
        name="activate",
        grid=(units,),
        in_specs=[unit(1, rank.shape[2]), whole(scale)] + [unit(slots, double)] * len(parts),
        out_specs=unit(slots, double // 2),
        out_shape=jax.ShapeDtypeStruct((units, slots, double // 2), BF16),
        cost_estimate=cost(10 * units * slots * double, 4 * units * slots * double),
    )(rank, scale, *parts)


def leave_kernel(groups, chained, expert_ref, rank_ref, weight_ref, act_ref, down_ref, *refs):
    del expert_ref
    before = refs[0] if chained else None
    outs, total_ref = refs[chained : chained + groups], refs[chained + groups]
    unit = pl.program_id(0)

    @pl.when(unit == 0)
    def _():
        total_ref[...] = before[...] if chained else jnp.zeros_like(total_ref)

    slots = act_ref.shape[1]
    value = dot(act_ref[0], down_ref[0]).astype(BF16)
    here = rank_ref[0] == iota((slots, rank_ref.shape[2]), 0, F32)
    blend = jnp.where(here, weight_ref[0], 0.0).astype(BF16)
    total_ref[...] += dot(blend, value, ((0,), (0,)))

    @pl.when(unit == pl.num_programs(0) - 1)
    def _():
        rows = outs[0].shape[0]
        for n, ref in enumerate(outs):
            ref[...] = total_ref[n * rows : (n + 1) * rows, :].astype(ref.dtype)


def leave(experts, rank, weight, act, w_down, before, groups):
    units, _, length = rank.shape
    hidden, width = w_down.shape[1:]
    unit = lambda *shape: pl.BlockSpec((1, *shape), lambda u, _: (u, 0, 0))
    down = pl.BlockSpec((1, hidden, width), lambda u, experts: (experts[u], 0, 0))
    chained = before is not None
    outs = [
        jax.ShapeDtypeStruct((length // groups, width), BF16 if n else F32)
        for n in range(groups)
    ]
    args = (rank, weight, act, w_down) + ((before,) if chained else ())
    return pl.pallas_call(
        functools.partial(leave_kernel, groups, chained),
        name="leave",
        grid_spec=pltpu.PrefetchScalarGridSpec(
            num_scalar_prefetch=1,
            grid=(units,),
            in_specs=[unit(1, length), unit(1, length), unit(*act.shape[1:]), down]
            + ([whole(before)] if chained else []),
            out_specs=[whole(o) for o in outs],
            scratch_shapes=[pltpu.VMEM((length, width), F32)],
        ),
        out_shape=outs,
        cost_estimate=cost(2 * units * act.shape[1] * width * hidden, 2 * units * width * hidden),
    )(experts, *args)


def shifted(value, axis, by):
    size = lax.axis_size(axis)
    return lax.ppermute(value, axis, [(i, (i + by) % size) for i in range(size)])


def crossed(value, axis, bit):
    return lax.ppermute(value, axis, [(i, i ^ bit) for i in range(lax.axis_size(axis))])


def from_source(value, k, j):
    if k == 0 and j == 0:
        return value
    data, tensor = lax.axis_size("dp"), lax.axis_size("tensor")
    pairs = [
        (d * tensor + t, (d + j) % data * tensor + (t + k) % tensor)
        for d in range(data)
        for t in range(tensor)
    ]
    return lax.ppermute(value, ("dp", "tensor"), pairs)


def chunks_of(tensor):
    if tensor < 3:
        return [[k] for k in range(tensor)]
    return [[0], list(range(1, tensor - 1)), [tensor - 1]]


def reversed_bits(size):
    order = [0]
    while len(order) < size:
        order = [2 * p for p in order] + [2 * p + 1 for p in order]
    return order


def body(
    ssm_in,
    gate_z,
    b_proj,
    c_proj,
    step_size,
    decay_rate,
    norm_gain,
    w_out,
    residual,
    moe_gain,
    expert_ids,
    route_weight,
    w_gate,
    w_up,
    w_down,
):
    data, tensor, parts = (lax.axis_size(a) for a in ("dp", "tensor", "expert"))
    channels_here = ssm_in.shape[1]
    head_dim = channels_here // step_size.shape[1]
    rows, features = residual.shape
    here = lax.axis_index("tensor")

    packed = jnp.concatenate([expert_ids.astype(F32).T, route_weight.astype(F32).T], axis=0)
    sources = [(k, j) for k in range(tensor) for j in range(data)]
    routes = {kj: from_source(packed, *kj) for kj in sources}

    xt, growth, ending, decay = scan_in(ssm_in, step_size, decay_rate, b_proj, head_dim)
    incoming = jnp.zeros_like(ending)
    for hop in range(data - 1):
        if hop:
            carried = incoming.astype(F32) * decay[0:1] + ending.astype(F32)
            sent = carried.astype(BF16)
        else:
            sent = ending
        incoming = lax.ppermute(sent, "dp", [(i, i + 1) for i in range(data - 1)])
    y, gate = scan_local(c_proj, b_proj, xt, gate_z, growth, head_dim)
    order = (here + jnp.arange(tensor, dtype=jnp.int32)) % tensor
    values, squares = project(
        order, c_proj, y, gate, incoming, norm_gain.reshape(1, -1), w_out
    )
    values = [v if k == 0 else shifted(v, "tensor", k) for k, v in enumerate(values)]
    squares = [v if k == 0 else shifted(v, "tensor", k) for k, v in enumerate(squares)]
    stream, sent, model_square = home(
        values, squares, residual, moe_gain.reshape(1, -1), channels_here * tensor
    )

    blocks = {}
    moving = sent
    for k in range(tensor):
        if k:
            moving = shifted(moving, "tensor", 1)
        for j in range(data):
            blocks[k, j] = moving if j == 0 else shifted(moving, "dp", j)
    bit = 1
    while bit < parts:
        model_square = model_square + crossed(model_square, "expert", bit)
        bit *= 2
    model_scale = lax.rsqrt(model_square / (features * parts) + EPSILON)
    scales = {kj: from_source(model_scale, *kj) for kj in sources}

    local = w_gate.shape[0]
    experts_all = local * data * tensor
    top = expert_ids.shape[1]
    slot_count = max(2, 7 * rows * top // (5 * experts_all))
    share = max(1, parts // local)
    several = max(1, local // parts)
    mine = lax.axis_index("expert")
    part = jnp.array(reversed_bits(parts), jnp.int32) ^ mine
    if share == 1:
        expert = (part[:, None] * several + jnp.arange(several, dtype=jnp.int32)).reshape(-1)
    else:
        expert = part // share
    units = expert.shape[0]
    first_expert = (lax.axis_index("dp") * tensor + here) * local
    named = (first_expert + expert).astype(F32)

    contributions = []
    for ks in chunks_of(tensor):
        chosen = [(k, j) for j in range(data) for k in ks]
        slots = slot_count * len(chosen) // share
        table = jnp.concatenate([routes[kj] for kj in chosen], axis=1)
        scale = jnp.concatenate([scales[kj] for kj in chosen], axis=1)[0:1]
        length = table.shape[1]
        match = table[:top, None, :] == named[None, :, None]
        routed = jnp.sum(match.astype(F32), axis=0)
        weight = jnp.sum(jnp.where(match, table[top:, None, :], 0.0), axis=0)
        shape = (length, length)
        before = (iota(shape, 0) < iota(shape, 1)).astype(BF16)
        rank = dot(routed.astype(BF16), before)
        if share > 1:
            rank = rank - ((part % share) * slots).astype(F32)[:, None]
        rank = jnp.where(routed > 0.0, rank, -1.0)[:, None, :]
        weight = weight[:, None, :]
        tokens = [blocks[kj] for kj in chosen]

        half = units // 2
        pieces = []
        if parts > 1:
            leaving = enter(expert[half:], rank[half:], tokens, w_gate, w_up, slots)
            arrived = crossed(leaving, "expert", 1)
            pieces = [enter(expert[:half], rank[:half], tokens, w_gate, w_up, slots), arrived]
        else:
            pieces = [enter(expert, rank, tokens, w_gate, w_up, slots)]
        bit, held = 2, half
        while bit < parts:
            held //= 2
            partial = sum(p[held : 2 * held].astype(F32) for p in pieces).astype(BF16)
            pieces.append(crossed(partial, "expert", bit))
            bit *= 2
        act = activate(rank, scale, pieces)
        while bit > 2:
            bit //= 2
            act = jnp.concatenate([act, crossed(act, "expert", bit)], axis=0)
        groups = data
        if parts > 1:
            other = crossed(act, "expert", 1)
            (partial,) = leave(expert[:half], rank[:half], weight[:half], act, w_down, None, 1)
            outs = leave(
                expert[half:], rank[half:], weight[half:], other, w_down, partial, groups
            )
        else:
            outs = leave(expert, rank, weight, act, w_down, None, groups)
        outs = [outs[0]] + [shifted(o, "dp", -j) for j, o in enumerate(outs) if j]
        for n, k in enumerate(ks):
            piece = sum(o[n * rows : (n + 1) * rows].astype(F32) for o in outs)
            if k:
                piece = shifted(piece.astype(BF16), "tensor", -k).astype(F32)
            contributions.append(piece)
    return (stream.astype(F32) + sum(contributions)).astype(BF16)


def solution(mesh):
    return jax.shard_map(
        body,
        mesh=mesh,
        in_specs=(
            P("dp", "tensor"),
            P("dp", "tensor"),
            P("dp", None),
            P("dp", None),
            P("dp", "tensor"),
            P("tensor"),
            P("tensor"),
            P("tensor", "expert"),
            P(("dp", "tensor"), "expert"),
            P("expert"),
            P(("dp", "tensor"), None),
            P(("dp", "tensor"), None),
            P(("dp", "tensor"), "expert", None),
            P(("dp", "tensor"), "expert", None),
            P(("dp", "tensor"), None, "expert"),
        ),
        out_specs=P(("dp", "tensor"), "expert"),
        check_vma=False,
    )
```

```python
import functools

import jax
import jax.numpy as jnp
from jax import lax
from jax.experimental import pallas as pl
from jax.experimental.pallas import tpu as pltpu
from jax.sharding import PartitionSpec as P

EPSILON = 1e-05
F32, BF16 = jnp.float32, jnp.bfloat16


def dot(a, b, dims=((1,), (0,))):
    return lax.dot_general(a, b, (dims, ((), ())), preferred_element_type=F32)


def iota(shape, dim, dtype=jnp.int32):
    return lax.broadcasted_iota(jnp.int32, shape, dim).astype(dtype)


def silu_of(value):
    return value / (1.0 + jnp.exp(-value))


def split3(value):
    hi = value.astype(BF16)
    rest = value - hi.astype(F32)
    mid = rest.astype(BF16)
    return hi, mid, (rest - mid.astype(F32)).astype(BF16)


def spread(value, head_dim, width, first):
    heads = value.shape[1]
    channel = iota((heads, width), 1) + first
    head = iota((heads, width), 0)
    low = head * head_dim
    member = ((channel >= low) & (channel < low + head_dim)).astype(F32).astype(BF16)
    return sum(dot(part, member) for part in split3(value))


def row_sums(square):
    ones = jnp.ones((8, square.shape[1]), BF16)
    hi = square.astype(BF16)
    lo = (square - hi.astype(F32)).astype(BF16)
    along = ((1,), (1,))
    return dot(ones, hi, along) + dot(ones, lo, along)


PARAMS = pltpu.CompilerParams(vmem_limit_bytes=8 << 20)


def cost(flops, read):
    return pl.CostEstimate(flops=int(flops), bytes_accessed=int(read), transcendentals=0)


def whole(array):
    return pl.BlockSpec(array.shape, lambda *_: (0,) * len(array.shape))


def scan_in_kernel(head_dim, x_ref, step_ref, rate_ref, b_ref, xt_ref, g_ref, s_ref, d_ref, a_ref):
    tile = pl.program_id(0)
    length = step_ref.shape[0]
    width = x_ref.shape[1]

    @pl.when(tile == 0)
    def _():
        step = step_ref[...]
        log_decay = -step * rate_ref[...]
        shape = (length, length)
        lower = (iota(shape, 0) >= iota(shape, 1)).astype(F32).astype(BF16)
        total = sum(dot(lower, part) for part in split3(log_decay))
        a_ref[...] = step * jnp.exp(-total)
        g_ref[...] = jnp.exp(total)

    first = tile * width
    scaled = x_ref[...].astype(F32) * spread(a_ref[...], head_dim, width, first)
    xt = scaled.astype(BF16)
    xt_ref[...] = xt
    ending = spread(g_ref[length - 8 : length, :], head_dim, width, first)[7:8, :]
    d_ref[...] = jnp.broadcast_to(ending, d_ref.shape)
    s_ref[...] = (dot(b_ref[...], xt, ((0,), (0,))) * ending).astype(BF16)


def scan_in(ssm_in, step_size, decay_rate, b_proj, head_dim):
    length, channels = ssm_in.shape
    heads, state = step_size.shape[1], b_proj.shape[1]
    width = min(256, channels)
    rate = decay_rate.reshape(1, heads)
    column = lambda rows: pl.BlockSpec((rows, width), lambda i: (0, i))
    return pl.pallas_call(
        functools.partial(scan_in_kernel, head_dim),
        name="scan_in",
        grid=(channels // width,),
        in_specs=[column(length), whole(step_size), whole(rate), whole(b_proj)],
        out_specs=[column(length), whole(step_size), column(state), column(8)],
        out_shape=[
            jax.ShapeDtypeStruct((length, channels), BF16),
            jax.ShapeDtypeStruct((length, heads), F32),
            jax.ShapeDtypeStruct((state, channels), BF16),
            jax.ShapeDtypeStruct((8, channels), F32),
        ],
        scratch_shapes=[pltpu.VMEM((length, heads), F32)],
        compiler_params=PARAMS,
        cost_estimate=cost(2 * length * channels * state, 4 * length * channels),
    )(ssm_in, step_size, rate, b_proj)


def scan_local_kernel(head_dim, c_ref, b_ref, xt_ref, z_ref, g_ref, y_ref, gate_ref, score_ref):
    tile = pl.program_id(0)
    length = c_ref.shape[0]
    width = xt_ref.shape[1]

    @pl.when(tile == 0)
    def _():
        score = dot(c_ref[...], b_ref[...], ((1,), (1,)))
        shape = (length, length)
        causal = iota(shape, 0) >= iota(shape, 1)
        score_ref[...] = jnp.where(causal, score, 0.0).astype(BF16)

    gate = spread(g_ref[...], head_dim, width, tile * width) * silu_of(z_ref[...].astype(F32))
    gate_ref[...] = gate
    y_ref[...] = dot(score_ref[...], xt_ref[...]) * gate


def scan_local(c_proj, b_proj, xt, gate_z, growth, head_dim):
    length, channels = xt.shape
    width = min(256, channels)
    column = pl.BlockSpec((length, width), lambda i: (0, i))
    out = jax.ShapeDtypeStruct((length, channels), F32)
    return pl.pallas_call(
        functools.partial(scan_local_kernel, head_dim),
        name="scan_local",
        grid=(channels // width,),
        in_specs=[whole(c_proj), whole(b_proj), column, column, whole(growth)],
        out_specs=[column, column],
        out_shape=[out, out],
        scratch_shapes=[pltpu.VMEM((length, length), BF16)],
        compiler_params=PARAMS,
        cost_estimate=cost(2 * length * channels * length, 12 * length * channels),
    )(c_proj, b_proj, xt, gate_z, growth)


def project_kernel(count, order_ref, c_ref, y_ref, gate_ref, s_ref, gain_ref, w_ref, *outs):
    del order_ref
    step = pl.program_id(0)
    gated = y_ref[...] + dot(c_ref[...], s_ref[...]) * gate_ref[...]
    squares = row_sums(gated * gated)
    value = dot((gated * gain_ref[...]).astype(BF16), w_ref[...])
    for k in range(count):

        @pl.when(step == k)
        def _(k=k):
            outs[k][...] = value.astype(outs[k].dtype)
            outs[count + k][...] = squares


def project(order, c_proj, y, gate, incoming, gain, w_out):
    count = order.shape[0]
    length, channels = y.shape
    rows, features = length // count, w_out.shape[1]
    block = lambda cols: pl.BlockSpec((rows, cols), lambda i, order: (order[i], 0))
    values = [
        jax.ShapeDtypeStruct((rows, features), BF16 if k else F32) for k in range(count)
    ]
    squares = [jax.ShapeDtypeStruct((8, rows), F32)] * count
    outs = pl.pallas_call(
        functools.partial(project_kernel, count),
        name="project",
        grid_spec=pltpu.PrefetchScalarGridSpec(
            num_scalar_prefetch=1,
            grid=(count,),
            in_specs=[block(c_proj.shape[1]), block(channels), block(channels)]
            + [whole(incoming), whole(gain), whole(w_out)],
            out_specs=[whole(s) for s in values + squares],
        ),
        out_shape=values + squares,
        compiler_params=PARAMS,
        cost_estimate=cost(2 * length * channels * features, 12 * length * channels),
    )(order, c_proj, y, gate, incoming, gain, w_out)
    return outs[:count], outs[count:]


def home_kernel(count, channels, *refs):
    values, squares = refs[:count], refs[count : 2 * count]
    residual_ref, stream_ref, model_ref = refs[2 * count], refs[-2], refs[-1]
    total = sum(ref[...].astype(F32) for ref in values)
    square = sum(ref[...] for ref in squares)
    scale = jnp.transpose(lax.rsqrt(square / channels + EPSILON))[:, 0:1]
    stream = (residual_ref[...].astype(F32) + total * scale).astype(BF16)
    stream_ref[...] = stream
    wide = stream.astype(F32)
    model_ref[...] = row_sums(wide * wide)


def home(values, squares, residual, channels, after):
    rows, features = residual.shape
    args = (*values, *squares, residual)
    out = jax.ShapeDtypeStruct((rows, features), BF16)
    model = jax.ShapeDtypeStruct((8, rows), F32)
    return pl.pallas_call(
        functools.partial(home_kernel, len(values), channels),
        name="home",
        in_specs=[resident()] * len(args) + [pl.BlockSpec(memory_space=pl.ANY)] * len(after),
        out_specs=[resident()] * 2,
        out_shape=[out, model],
        compiler_params=PARAMS,
        cost_estimate=cost(rows * features * 10, 16 * rows * features),
    )(*args, *after)


def normalize_kernel(features, stream_ref, gain_ref, *refs):
    squares, out_ref = refs[:-1], refs[-1]
    square = sum(ref[...] for ref in squares)
    scale = jnp.transpose(lax.rsqrt(square / features + EPSILON))[:, 0:1]
    out_ref[...] = (stream_ref[...].astype(F32) * scale * gain_ref[...]).astype(BF16)


def normalize(stream, gain, squares, features):
    return pl.pallas_call(
        functools.partial(normalize_kernel, features),
        name="normalize",
        out_shape=jax.ShapeDtypeStruct(stream.shape, BF16),
        compiler_params=PARAMS,
        cost_estimate=cost(4 * stream.size, 4 * stream.size),
    )(stream, gain, *squares)


def paired_kernel(own_ref, *refs):
    out_ref = refs[-1]
    total = own_ref[...] + sum(ref[...].astype(F32) for ref in refs[:-1])
    out_ref[...] = total.astype(out_ref.dtype)


def paired(own, others, kind):
    return pl.pallas_call(
        paired_kernel,
        name="paired",
        out_shape=jax.ShapeDtypeStruct(own.shape, kind),
        compiler_params=PARAMS,
        cost_estimate=cost(2 * own.size, 8 * own.size),
    )(own, *others)


def resident():
    return pl.BlockSpec(memory_space=pltpu.VMEM)


def routes_kernel(chunks, slots, top, table_ref, named_ref, *outs):
    tables = [table_ref[s] for s in range(table_ref.shape[0])]
    named, shift = named_ref[:, 0:1], named_ref[:, 1:2]
    for c, sources in enumerate(chunks):
        table = jnp.concatenate([tables[s] for s in sources], axis=1)
        length = table.shape[1]
        routed = jnp.zeros((named.shape[0], length), F32)
        weight = jnp.zeros((named.shape[0], length), F32)
        for k in range(top):
            match = table[k : k + 1, :] == named
            routed = jnp.where(match, 1.0, routed)
            weight = jnp.where(match, table[top + k : top + k + 1, :], weight)
        shape = (length, length)
        before = (iota(shape, 0) < iota(shape, 1)).astype(F32).astype(BF16)
        rank = dot(routed.astype(BF16), before) - shift * slots[c]
        outs[2 * c][...] = jnp.where(routed > 0.0, rank, -1.0)
        outs[2 * c + 1][...] = weight


def routes_of(table, named, chunks, slots, top):
    units, rows = named.shape[0], table.shape[2]
    outs = [
        jax.ShapeDtypeStruct((units, rows * len(sources)), F32)
        for sources in chunks
        for _ in range(2)
    ]
    flat = pl.pallas_call(
        functools.partial(routes_kernel, chunks, slots, top),
        name="routes",
        out_shape=outs,
        compiler_params=PARAMS,
        cost_estimate=cost(1e7, 1e6),
    )(table, named)
    return list(zip(flat[0::2], flat[1::2]))


def held_near_kernel(count, *refs):
    sources, outs, sems = refs[:count], refs[count : 2 * count], refs[-1]
    copies = [
        pltpu.make_async_copy(source.at[e], out.at[e], sems.at[n, e])
        for n, (source, out) in enumerate(zip(sources, outs))
        for e in range(source.shape[0])
    ]
    for copy in copies:
        copy.start()
    for copy in copies:
        copy.wait()


def held_near(arrays):
    count = len(arrays)
    return pl.pallas_call(
        functools.partial(held_near_kernel, count),
        name="held_near",
        in_specs=[pl.BlockSpec(memory_space=pltpu.HBM)] * count,
        out_specs=[resident()] * count,
        out_shape=[pltpu.VMEM(a.shape, a.dtype) for a in arrays],
        scratch_shapes=[pltpu.SemaphoreType.DMA((count, arrays[0].shape[0]))],
        compiler_params=PARAMS,
        cost_estimate=cost(0, sum(2 * a.size for a in arrays)),
    )(*arrays)


def place(rank_ref, units, slots):
    length = rank_ref.shape[1]
    slot = iota((slots, length), 0, F32)
    return [rank_ref[u : u + 1, :] == slot for u in units]


ANYWHERE = pl.BlockSpec(memory_space=pl.ANY)


def enter_kernel(blocks, units, added, expert_ref, rank_ref, *refs):
    tokens = refs[:blocks]
    gate_w, up_w = refs[blocks : blocks + 2]
    extra_ref = refs[blocks + 2] if added else None
    out_ref, token_ref = refs[-2:]
    rows = tokens[0].shape[0]
    for n, ref in enumerate(tokens):
        token_ref[n * rows : (n + 1) * rows, :] = ref[...]
    slots, hidden = out_ref.shape[1], gate_w.shape[2]
    here = jnp.concatenate([p.astype(F32) for p in place(rank_ref, units, slots)], axis=0)
    rows_in = dot(here.astype(BF16), token_ref[...])
    for n, u in enumerate(units):
        value = rows_in[n * slots : (n + 1) * slots].astype(BF16)
        expert = expert_ref[u]
        gate, up = dot(value, gate_w[expert]), dot(value, up_w[expert])
        if added:
            first = added - 1
            gate = gate + extra_ref[first + n, :, :hidden].astype(F32)
            up = up + extra_ref[first + n, :, hidden:].astype(F32)
        out_ref[n, :, :hidden] = gate.astype(BF16)
        out_ref[n, :, hidden:] = up.astype(BF16)


def enter(experts, rank, units, tokens, w_gate, w_up, slots, after, extra=None, first=0):
    length = rank.shape[1]
    width, hidden = w_gate.shape[1:]
    count = len(units)
    added = 0 if extra is None else first + 1
    args = (rank, *tokens, w_gate, w_up) + (() if extra is None else (extra,))
    return pl.pallas_call(
        functools.partial(enter_kernel, len(tokens), units, added),
        name="enter",
        in_specs=[pl.BlockSpec(memory_space=pltpu.SMEM)]
        + [resident()] * len(args)
        + [ANYWHERE] * len(after),
        out_specs=resident(),
        scratch_shapes=[pltpu.VMEM((length, width), BF16)],
        out_shape=jax.ShapeDtypeStruct((count, slots, 2 * hidden), BF16),
        compiler_params=PARAMS,
        cost_estimate=cost(1.5e9 * count, 2e6),
    )(experts, *args, *after)


def activate_kernel(count, pieces, *refs):
    parts, out_ref = refs[:pieces], refs[-1]
    hidden = out_ref.shape[2]
    for n in range(count):
        total = sum(ref[n].astype(F32) for ref in parts)
        out_ref[n] = (silu_of(total[:, :hidden]) * total[:, hidden:]).astype(BF16)


def activate(count, parts, after):
    slots, double = parts[0].shape[1:]
    return pl.pallas_call(
        functools.partial(activate_kernel, count, len(parts)),
        name="activate",
        in_specs=[resident()] * len(parts) + [ANYWHERE] * len(after),
        out_specs=resident(),
        out_shape=jax.ShapeDtypeStruct((count, slots, double // 2), BF16),
        compiler_params=PARAMS,
        cost_estimate=cost(1e8, 2e6),
    )(*parts, *after)


def leave_kernel(units, pieces, chained, count, expert_ref, rank_ref, weight_ref, down_ref, *refs):
    acts = [(ref, n) for ref in refs[:pieces] for n in range(ref.shape[0])]
    outs, value_ref = refs[-1 - count : -1], refs[-1]
    slots = refs[0].shape[1]
    step = pl.program_id(0)
    for n, (ref, m) in enumerate(acts):

        @pl.when(step == n)
        def _(n=n, ref=ref, m=m):
            value_ref[n * slots : (n + 1) * slots, :] = dot(ref[m], down_ref[0]).astype(BF16)

    @pl.when(step == len(acts) - 1)
    def _():
        blends = [
            jnp.where(here, weight_ref[u : u + 1, :], 0.0)
            for u, here in zip(units, place(rank_ref, units, slots))
        ]
        blend = jnp.concatenate(blends, axis=0).astype(BF16)
        total = dot(blend, value_ref[...], ((0,), (0,)))
        rows = outs[0].shape[0]
        for n, ref in enumerate(outs):
            piece = total[n * rows : (n + 1) * rows]
            if chained:
                piece = piece + refs[pieces][n * rows : (n + 1) * rows, :]
            ref[...] = piece.astype(ref.dtype)


def leave(experts, rank, weight, units, acts, w_down, after, before, kinds):
    length = rank.shape[1]
    hidden, width = w_down.shape[1:]
    slots = acts[0].shape[1]
    chained = before is not None
    outs = [jax.ShapeDtypeStruct((length // len(kinds), width), kind) for kind in kinds]
    args = (rank, weight, w_down, *acts) + ((before,) if chained else ())
    down = pl.BlockSpec((1, hidden, width), lambda u, experts: (experts[units[0] + u], 0, 0))
    return pl.pallas_call(
        functools.partial(leave_kernel, units, len(acts), int(chained), len(kinds)),
        name="leave",
        grid_spec=pltpu.PrefetchScalarGridSpec(
            num_scalar_prefetch=1,
            grid=(len(units),),
            in_specs=[resident()] * 2
            + [down]
            + [resident()] * (len(args) - 3)
            + [ANYWHERE] * len(after),
            out_specs=[resident()] * len(kinds),
            scratch_shapes=[pltpu.VMEM((len(units) * slots, width), BF16)],
        ),
        out_shape=outs,
        compiler_params=PARAMS,
        cost_estimate=cost(0.7e9 * len(units), 2 * len(units) * hidden * width),
    )(experts, *args, *after)


def crossed(value, axis, bits):
    if bits == 0:
        return value
    return lax.ppermute(value, axis, [(i, i ^ bits) for i in range(lax.axis_size(axis))])


def gathered(value):
    value = value[None]
    for axis in ("dp", "tensor"):
        bit = 1
        while bit < lax.axis_size(axis):
            value = jnp.concatenate([value, crossed(value, axis, bit)], axis=0)
            bit *= 2
    return value


def chunks_of(tensor):
    if tensor < 3:
        return [[k] for k in range(tensor)]
    return [[0], list(range(1, tensor - 1)), [tensor - 1]]


def reversed_bits(size):
    order = [0]
    while len(order) < size:
        order = [2 * p for p in order] + [2 * p + 1 for p in order]
    return order


def body(
    ssm_in,
    gate_z,
    b_proj,
    c_proj,
    step_size,
    decay_rate,
    norm_gain,
    w_out,
    residual,
    moe_gain,
    expert_ids,
    route_weight,
    w_gate,
    w_up,
    w_down,
):
    data, tensor, parts = (lax.axis_size(a) for a in ("dp", "tensor", "expert"))
    channels_here = ssm_in.shape[1]
    head_dim = channels_here // step_size.shape[1]
    rows, features = residual.shape
    here = lax.axis_index("tensor")

    xt, growth, ending, decay = scan_in(ssm_in, step_size, decay_rate, b_proj, head_dim)
    incoming = jnp.zeros_like(ending)
    for hop in range(data - 1):
        if hop:
            carried = incoming.astype(F32) * decay[0:1] + ending.astype(F32)
            sent = carried.astype(BF16)
        else:
            sent = ending
        incoming = lax.ppermute(sent, "dp", [(i, i + 1) for i in range(data - 1)])
    y, gate = scan_local(c_proj, b_proj, xt, gate_z, growth, head_dim)
    order = here ^ jnp.arange(tensor, dtype=jnp.int32)
    values, squares = project(
        order, c_proj, y, gate, incoming, norm_gain.reshape(1, -1), w_out
    )
    table = jnp.concatenate([expert_ids.astype(F32).T, route_weight.astype(F32).T], axis=0)
    table, ending = lax.optimization_barrier((table, ending))
    table = gathered(table)
    values = [crossed(v, "tensor", k) for k, v in enumerate(values)]
    squares = [crossed(v, "tensor", k) for k, v in enumerate(squares)]

    local = w_gate.shape[0]
    experts_all = local * data * tensor
    top = expert_ids.shape[1]
    slot_count = max(2, 7 * rows * top // (5 * experts_all))
    share = max(1, parts // local)
    several = max(1, local // parts)
    part = jnp.array(reversed_bits(parts), jnp.int32) ^ lax.axis_index("expert")
    if share == 1:
        expert = (part[:, None] * several + jnp.arange(several, dtype=jnp.int32)).reshape(-1)
        shift = jnp.zeros_like(expert)
    else:
        expert = part // share
        shift = part % share
    units = expert.shape[0]
    first_expert = (lax.axis_index("dp") * tensor + here) * local
    named = jnp.stack([(first_expert + expert).astype(F32), shift.astype(F32)], axis=1)
    gain = moe_gain.reshape(1, -1)
    chunks = chunks_of(tensor)
    sources = [[k * data + j for j in range(data) for k in ks] for ks in chunks]
    slots_of = [slot_count * len(chosen) // share for chosen in sources]
    own = values[0]
    routes = routes_of(table, named, sources, slots_of, top)
    (own, expert, gain, routes, w_gate, w_up, w_down) = lax.optimization_barrier(
        (own, expert, gain, routes, w_gate, w_up, w_down)
    )
    w_gate, w_up, w_down = [held_near((w,))[0] for w in (w_gate, w_up)] + [w_down]
    values[0] = own
    w_down = pltpu.with_memory_space_constraint(w_down, pltpu.HBM)
    after = (w_gate, w_up, routes[0][0])
    stream, model = home(values, squares, residual, channels_here * tensor, after)
    model = [crossed(model, "expert", e) for e in range(parts)]
    sent = normalize(stream, gain, model, features * parts)

    blocks = {}
    for k in range(tensor):
        moved = crossed(sent, "tensor", k)
        for j in range(data):
            blocks[k * data + j] = crossed(moved, "dp", j)

    half = units // 2 if parts > 1 else units
    finished = units // parts
    lower, upper = list(range(half)), list(range(half, units))
    count = len(chunks)
    last, pieces, acts, contributions = [], {}, {}, []

    def entry(c):
        tokens = [blocks[s] for s in sources[c]]

        def into(us, *more):
            out = enter(
                expert, routes[c][0], list(us), tokens, w_gate, w_up, slots_of[c], last[:], *more
            )
            last[:] = [out]
            return out

        if parts == 1:
            pieces[c] = [into(lower)]
            return
        arrived = crossed(into(upper), "expert", 1)
        pieces[c], bit, held = [into(range(finished)), arrived], 2, half
        while bit < parts:
            held //= 2
            partial = into(range(held, 2 * held), arrived, held)
            for p in pieces[c][2:]:
                partial = (partial.astype(F32) + p[held : 2 * held].astype(F32)).astype(BF16)
            pieces[c].append(crossed(partial, "expert", bit))
            bit *= 2

    def middle(c):
        act = activate(finished, pieces[c], last[:])
        last[:] = [act]
        acts[c], bit = [act], parts
        while bit > 1:
            bit //= 2
            acts[c] = acts[c] + [crossed(a, "expert", bit) for a in acts[c]]

    def leaving(c):
        ks, (rank, weight) = chunks[c], routes[c]

        def out_of(us, pieces, *more):
            outs = leave(expert, rank, weight, us, pieces, w_down, last[:], *more)
            last[:] = outs[:1]
            return outs

        kinds = [BF16 if j else F32 for j in range(data) for _ in ks]
        if parts > 1:
            near, far = acts[c][: parts // 2], acts[c][parts // 2 :]
            (partial,) = out_of(lower, near, None, [F32])
            outs = out_of(upper, far, partial, kinds)
        else:
            outs = out_of(lower, acts[c], None, kinds)
        for n, k in enumerate(ks):
            others = [crossed(outs[j * len(ks) + n], "dp", j) for j in range(1, data)]
            piece = paired(outs[n], others, BF16 if k else F32)
            contributions.append(crossed(piece, "tensor", k))

    for c in range(count + 2):
        if c < count:
            entry(c)
        if 0 <= c - 2 < count:
            leaving(c - 2)
        if 0 <= c - 1 < count:
            middle(c - 1)
    total = sum(c.astype(F32) for c in contributions)
    return (stream.astype(F32) + total).astype(BF16)


def solution(mesh):
    return jax.shard_map(
        body,
        mesh=mesh,
        in_specs=(
            P("dp", "tensor"),
            P("dp", "tensor"),
            P("dp", None),
            P("dp", None),
            P("dp", "tensor"),
            P("tensor"),
            P("tensor"),
            P("tensor", "expert"),
            P(("dp", "tensor"), "expert"),
            P("expert"),
            P(("dp", "tensor"), None),
            P(("dp", "tensor"), None),
            P(("dp", "tensor"), "expert", None),
            P(("dp", "tensor"), "expert", None),
            P(("dp", "tensor"), None, "expert"),
        ),
        out_specs=P(("dp", "tensor"), "expert"),
        check_vma=False,
    )
```
